32 devices in a mesh: tx: 2 (over y), ty: 4 (over z), sl: 4 (over x, core).
Axes of the slice: x: 2, y: 2, z: 4, core: 2. Of those that a mesh axis runs over, the one named last changes fastest.
Arguments:
- object_field: float32 [8, 2, 512, 1024], P('sl', None, 'tx', 'ty'), may hold values from -0.4 to 1.2, as said below
- illumination: float32 [2, 256, 256], replicated, may hold values from -5 to 5
- positions: int32 [2, 4, 1, 2], P('tx', 'ty'), may hold values from 0 to 255
- measured: float32 [2, 4, 1, 256, 256], P('tx', 'ty'), may hold values from 0.05 to 1.5
Outputs:
- updated: float32 [8, 2, 512, 1024], P('sl', None, 'tx', 'ty')
The draws below stay inside these ranges and needn't reach their ends.
Inputs may be any that keep to these rules, and one draw needn't show every extreme that they name: `object_field`: real parts lie between 0.6 and 1.2, imaginary parts between -0.4 and 0.4.
All inputs are finite; a program needn't handle non-finite values.
Results may differ from the reference program's by a relative error of at most 0.0003.
Values sent between devices are 32-bit elements; how exact they have to be, the bound alone decides.
A program may use at most 128 MiB of HBM per device.

```python
import math
import jax
import jax.numpy as jnp
from jax import lax

TILE = 256
PW = 256
HALF = 128
SLICES = 8
PROBES = 1
TILES_X = 2
TILES_Y = 4
NX = 512
NY = 1024


def draw_object_field(key, part):
    key_real, key_imag = jax.random.split(key)
    shape_full = (SLICES, NX, NY)
    real_part = 0.9 + 0.12 * jnp.clip(jax.random.normal(key_real, shape_full, jnp.float32), -2.5, 2.5)
    imag_part = 0.15 * jnp.clip(jax.random.normal(key_imag, shape_full, jnp.float32), -2.5, 2.5)
    return jnp.stack([real_part, imag_part], axis=1)


def set_ends(entries, own_key, low, top_value):
    dims = entries.shape
    spot = [jax.random.randint(jax.random.fold_in(own_key, axis), (), 0, dims[axis]) for axis in range(len(dims))]
    entries = entries.at[tuple(spot)].set(low)
    longest = dims.index(max(dims))
    spot[longest] = (spot[longest] + 1) % dims[longest]
    return entries.at[tuple(spot)].set(top_value)


def shard_levels(stream_key, shape, pieces, low, high):
    level = 1.0
    for position, blocks in pieces:
        draws = jax.random.uniform(jax.random.fold_in(jax.random.fold_in(stream_key, 6), position), (blocks,), jnp.float32, low / len(pieces), high / len(pieces))
        level = level * jnp.repeat(jnp.exp(draws), shape[position] // blocks).reshape((-1,) + (1,) * (len(shape) - 1 - position))
    return level


def bell_draw(key, extent, scale, most, kind=jnp.bfloat16):
    entries = scale * jax.random.normal(key, extent, jnp.float32)
    return jnp.clip(entries, min=-most, max=most).astype(kind)


def setup_inputs(seed: int = 0) -> dict:
    seeds = jax.random.split(jax.random.key(seed), 5)
    return {
        "object_field": draw_object_field(jax.random.fold_in(seeds[4], 71), 0),
        "illumination": bell_draw(seeds[1], (2, PW, PW), 1.0, 5.0, jnp.float32),
        "positions": set_ends(jax.random.randint(seeds[2], (TILES_X, TILES_Y, PROBES, 2), 0, TILE), jax.random.fold_in(seeds[2], 1), 0, TILE - 1).astype(jnp.int32),
        "measured": jnp.clip(jnp.exp(math.log(1.5) - 3.4011974 * jax.random.uniform(seeds[3], (TILES_X, TILES_Y, PROBES, PW, PW), jnp.float32) ** shard_levels(seeds[3], (TILES_X, TILES_Y, PROBES, PW, PW), ((0, 2), (1, 4)), -0.2, 0.2)), 0.05, 1.5),
    }


PRECISE = lax.Precision.HIGHEST
STEP_SIZE = 0.5

def from_left(matrix, wave_field):

    def product(left_matrix, right_matrix):
        return jnp.einsum('jk,bkl->bjl', left_matrix, right_matrix, precision=PRECISE)
    real_m, imag_m = (matrix[0], matrix[1])
    real_w, imag_w = (wave_field[:, 0], wave_field[:, 1])
    return jnp.stack([product(real_m, real_w) - product(imag_m, imag_w), product(real_m, imag_w) + product(imag_m, real_w)], axis=1)

def from_right(wave_field, matrix):

    def product(left_matrix, right_matrix):
        return jnp.einsum('bjk,kl->bjl', left_matrix, right_matrix, precision=PRECISE)
    real_m, imag_m = (matrix[0], matrix[1])
    real_w, imag_w = (wave_field[:, 0], wave_field[:, 1])
    return jnp.stack([product(real_w, real_m) - product(imag_w, imag_m), product(real_w, imag_m) + product(imag_w, real_m)], axis=1)

def sandwich(matrix, wave_field):
    return from_right(from_left(matrix, wave_field), matrix)

def times_plain(first_term, second_term):
    real_a, imag_a = (first_term[..., 0, :, :], first_term[..., 1, :, :])
    real_b, imag_b = (second_term[..., 0, :, :], second_term[..., 1, :, :])
    return jnp.stack([real_a * real_b - imag_a * imag_b, real_a * imag_b + imag_a * real_b], axis=-3)

def times_conj(first_term, second_term):
    real_a, imag_a = (first_term[..., 0, :, :], first_term[..., 1, :, :])
    real_b, imag_b = (second_term[..., 0, :, :], second_term[..., 1, :, :])
    return jnp.stack([real_a * real_b + imag_a * imag_b, real_a * imag_b - imag_a * real_b], axis=-3)

def build_tables(length):
    indices = jnp.arange(length, dtype=jnp.int32)
    products = indices[:, None] * indices[None, :] % length
    angles = products.astype(jnp.float32) * (-2.0 * math.pi / length)
    factor = 1.0 / math.sqrt(length)
    forward = jnp.stack([jnp.cos(angles), jnp.sin(angles)]) * factor
    backward = jnp.stack([jnp.cos(angles), -jnp.sin(angles)]) * factor
    shifted = jnp.where(indices < length // 2, indices, indices - length)
    phases = (shifted * shifted % (4 * length)).astype(jnp.float32) * (-math.pi / (2 * length))
    cos_row = jnp.cos(phases)[None, :]
    sin_row = jnp.sin(phases)[None, :]
    columns = jnp.stack([backward[0] * cos_row - backward[1] * sin_row, backward[0] * sin_row + backward[1] * cos_row])
    spread = from_left(columns, forward[None])[0]
    spread_conj = jnp.stack([spread[0], -spread[1]])
    return (forward, backward, spread, spread_conj)

def detector_gradient(wave_field, measured_part, forward, backward):
    farfield = sandwich(forward, wave_field)
    intensity = farfield[:, 0] * farfield[:, 0] + farfield[:, 1] * farfield[:, 1]
    residual = (intensity - measured_part)[:, None]
    return sandwich(backward, residual * farfield)

def wrap_fold(padded_grad, axis_dim):
    full_length = padded_grad.shape[axis_dim]
    tile_length = full_length - 2 * HALF
    middle = lax.slice_in_dim(padded_grad, HALF, HALF + tile_length, axis=axis_dim)
    upper_rim = lax.slice_in_dim(padded_grad, 0, HALF, axis=axis_dim)
    lower_rim = lax.slice_in_dim(padded_grad, full_length - HALF, full_length, axis=axis_dim)
    upper_pad = [(0, 0)] * padded_grad.ndim
    lower_pad = [(0, 0)] * padded_grad.ndim
    upper_pad[axis_dim] = (tile_length - HALF, 0)
    lower_pad[axis_dim] = (0, tile_length - HALF)
    return middle + jnp.pad(upper_rim, upper_pad) + jnp.pad(lower_rim, lower_pad)

def reference(object_field, illumination, positions, measured):
    forward, backward, spread, spread_conj = build_tables(PW)
    padded = jnp.pad(object_field, ((0, 0), (0, 0), (HALF, HALF), (HALF, HALF)), mode='wrap')
    tile_rows = jnp.arange(TILES_X, dtype=jnp.int32)[:, None, None] * TILE
    tile_cols = jnp.arange(TILES_Y, dtype=jnp.int32)[None, :, None] * TILE
    row_starts = (positions[..., 0] + tile_rows).reshape(-1).astype(jnp.int32)
    col_starts = (positions[..., 1] + tile_cols).reshape(-1).astype(jnp.int32)
    flat_measured = measured.reshape(-1, PW, PW)

    def visit(gradient_sum, scan_items):
        row_start, col_start, measured_one = scan_items
        anchor = jnp.int32(0)
        windows = lax.dynamic_slice(padded, (anchor, anchor, row_start, col_start), (SLICES, 2, PW, PW))
        wave_field = illumination[None]
        saved_waves = []
        for layer_index in range(SLICES):
            saved_waves.append(wave_field)
            wave_field = sandwich(spread, times_plain(windows[layer_index][None], wave_field))
        adjoint_wave = detector_gradient(wave_field, measured_one[None], forward, backward)
        contribs = [None] * SLICES
        for layer_index in reversed(range(SLICES)):
            inner_grad = sandwich(spread_conj, adjoint_wave)
            contribs[layer_index] = times_conj(saved_waves[layer_index], inner_grad)[0]
            adjoint_wave = times_conj(windows[layer_index][None], inner_grad)
        stacked = jnp.stack(contribs)
        current = lax.dynamic_slice(gradient_sum, (anchor, anchor, row_start, col_start), (SLICES, 2, PW, PW))
        gradient_sum = lax.dynamic_update_slice(gradient_sum, current + stacked, (anchor, anchor, row_start, col_start))
        return (gradient_sum, None)
    gradient_sum = jnp.zeros(padded.shape, jnp.float32)
    gradient_sum, unused = lax.scan(visit, gradient_sum, (row_starts, col_starts, flat_measured))
    gradient = wrap_fold(wrap_fold(gradient_sum, 2), 3)
    return object_field - STEP_SIZE * gradient
```

```python
import functools

import jax
import jax.numpy as jnp
import ml_dtypes
import numpy as np
from jax import lax
from jax.experimental import pallas as pl
from jax.experimental.pallas import tpu as pltpu
from jax.sharding import PartitionSpec as P

STEP_SIZE = 0.5
MESH = pl.DeviceIdType.MESH


def high_low(x):
    high = x.astype(np.float32).astype(ml_dtypes.bfloat16)
    low = (x - high.astype(np.float64)).astype(np.float32).astype(ml_dtypes.bfloat16)
    return high, low


def build_tables(length):
    k = np.arange(length)
    angles = (np.outer(k, k) % length) * (-2.0 * np.pi / length)
    forward = np.exp(1j * angles) / np.sqrt(length)
    q = np.where(k < length // 2, k, k - length)
    phases = np.exp(-1j * np.pi * (q * q % (4 * length)) / (2 * length))
    spread = (np.conj(forward) * phases[None, :]) @ forward
    both = []
    for matrix in (spread, forward):
        real_h, real_l = high_low(matrix.real)
        imag_h, imag_l = high_low(matrix.imag)
        both.append(np.stack([real_h, imag_h, real_l, imag_l]))
    return np.stack(both)


def split(x):
    high = x.astype(jnp.bfloat16)
    low = (x - high.astype(jnp.float32)).astype(jnp.bfloat16)
    return high, low


def dot(a, b):
    return jnp.dot(a, b, preferred_element_type=jnp.float32)


def kernel(
    counts,
    obj,
    ill,
    pos,
    meas,
    tab,
    out,
    t_left,
    t_right,
    ybuf,
    zs,
    zr,
    win,
    psi,
    adj,
    term,
    gzs,
    gzr,
    gys,
    gyr,
    posbuf,
    y_s,
    y_r,
    z_s,
    z_r,
    gz_s,
    gz_r,
    gy_s,
    gy_r,
    p_s,
    p_r,
    w_s,
    w_r,
):
    nx, ny, ns = counts
    layers = obj.shape[0]
    width = obj.shape[-1]
    half = width // 2
    x = lax.axis_index("tx")
    y = lax.axis_index("ty")
    s_me = lax.axis_index("sl")
    last = ns - 1
    up = (lax.rem(x + nx - 1, nx), y, s_me)
    down = (lax.rem(x + 1, nx), y, s_me)
    left = (x, lax.rem(y + ny - 1, ny), s_me)
    right = (x, lax.rem(y + 1, ny), s_me)
    after = (x, y, jnp.minimum(s_me + 1, last))
    before = (x, y, jnp.maximum(s_me - 1, 0))
    top, bottom = pl.ds(0, half), pl.ds(half, half)

    barrier = pltpu.get_barrier_semaphore()
    for there in (up, down, left, right):
        pl.semaphore_signal(barrier, inc=1, device_id=there, device_id_type=MESH)

    @pl.when(s_me > 0)
    def _():
        pl.semaphore_signal(barrier, inc=1, device_id=before, device_id_type=MESH)

    @pl.when(s_me < last)
    def _():
        pl.semaphore_signal(barrier, inc=1, device_id=after, device_id_type=MESH)

    ends = jnp.where(s_me > 0, 1, 0) + jnp.where(s_me < last, 1, 0)
    pl.semaphore_wait(barrier, 4 + ends)

    def remote(src, dst, send, recv, there):
        return pltpu.make_async_remote_copy(
            src_ref=src,
            dst_ref=dst,
            send_sem=send,
            recv_sem=recv,
            device_id=there,
            device_id_type=MESH,
        )

    def pos_copies():
        return [
            remote(pos, posbuf.at[0], p_s.at[0], p_r.at[0], right),
            remote(pos, posbuf.at[1], p_s.at[1], p_r.at[1], left),
        ]

    def y_copies(s):
        return [
            remote(obj.at[s, :, top], ybuf.at[s, :, top], y_s.at[s, 0], y_r.at[s, 0], up),
            remote(obj.at[s, :, bottom], ybuf.at[s, :, bottom], y_s.at[s, 1], y_r.at[s, 1], down),
        ]

    def z_copies(s):
        return [
            remote(zs.at[s, 0], zr.at[s, 0], z_s.at[s, 0], z_r.at[s, 0], left),
            remote(zs.at[s, 1], zr.at[s, 1], z_s.at[s, 1], z_r.at[s, 1], right),
        ]

    def gz_copies(s):
        return [
            remote(gzs.at[s, 0], gzr.at[s, 0], gz_s.at[s, 0], gz_r.at[s, 0], right),
            remote(gzs.at[s, 1], gzr.at[s, 1], gz_s.at[s, 1], gz_r.at[s, 1], left),
        ]

    def gy_copies(s):
        return [
            remote(gys.at[s, :, top], gyr.at[s, :, top], gy_s.at[s, 0], gy_r.at[s, 0], down),
            remote(gys.at[s, :, bottom], gyr.at[s, :, bottom], gy_s.at[s, 1], gy_r.at[s, 1], up),
        ]

    def wave_copy():
        return remote(psi.at[layers], psi.at[0], w_s.at[0], w_r.at[0], after)

    def adj_copy():
        return remote(adj.at[0], adj.at[layers], w_s.at[1], w_r.at[1], before)

    for copy in pos_copies():
        copy.start()
    for s in range(layers):
        for copy in y_copies(s):
            copy.start()

    for which in range(2):
        for part in range(2):
            real = tab[which, 2 * part]
            imag = tab[which, 2 * part + 1]
            t_right[which, part, 0:width, 0:width] = real
            t_right[which, part, 0:width, width : 2 * width] = imag
            t_right[which, part, width : 2 * width, 0:width] = -imag
            t_right[which, part, width : 2 * width, width : 2 * width] = real
            t_left[which, part, 0:width, 0:width] = real
            t_left[which, part, 0:width, width : 2 * width] = -imag
            t_left[which, part, width : 2 * width, 0:width] = imag
            t_left[which, part, width : 2 * width, width : 2 * width] = real

    @pl.when(s_me == 0)
    def _():
        psi[0] = ill[...]

    def own_rows(row):
        cells = lax.broadcasted_iota(jnp.int32, (width, half), 0)
        return (cells >= row - half) & (cells < row + half)

    def own_cols(side):
        cells = lax.broadcasted_iota(jnp.int32, (width, half), 1) + side * half
        col = pos[1, 0:1, 0:half]
        return (cells >= col - half) & (cells < col + half)

    def my_rows():
        return own_rows(pos[0, 0:1, 0:half])

    def their_rows(slot):
        return own_rows(posbuf[slot, 0, 0:1, 0:half])

    sides = (slice(0, half), slice(half, width))

    for copy in pos_copies():
        copy.wait_recv()

    def send_columns(s, carry):
        for copy in y_copies(s):
            copy.wait_recv()
        for side in range(2):
            rows = their_rows(side)
            for part in range(2):
                zs[s, side, part] = jnp.where(
                    rows, obj[s, part, :, sides[side]], ybuf[s, part, :, sides[side]]
                )
        for copy in z_copies(s):
            copy.start()
        return carry

    lax.fori_loop(0, layers, send_columns, 0)

    def sandwich(which, real, imag):
        high, low = split(jnp.concatenate([real, imag], axis=0))
        t_h, t_l = t_left[which, 0], t_left[which, 1]
        done = dot(t_h, high) + dot(t_h, low) + dot(t_l, high)
        high, low = split(jnp.concatenate([done[:width], done[width:]], axis=1))
        t_h, t_l = t_right[which, 0], t_right[which, 1]
        done = dot(high, t_h) + dot(low, t_h) + dot(high, t_l)
        return done[:, :width], done[:, width:]

    def table_of(s):
        return jnp.where((s_me == last) & (s == layers - 1), 1, 0)

    def go_forward(s, carry):
        for copy in z_copies(s):
            copy.wait_recv()
        rows = my_rows()
        for side in range(2):
            cols = own_cols(side)
            for part in range(2):
                mixed = jnp.where(
                    rows, obj[s, part, :, sides[side]], ybuf[s, part, :, sides[side]]
                )
                win[s, part, :, sides[side]] = jnp.where(cols, mixed, zr[s, side, part])

        @pl.when((s == 0) & (s_me > 0))
        def _():
            wave_copy().wait_recv()

        w_re, w_im = win[s, 0], win[s, 1]
        p_re, p_im = psi[s, 0], psi[s, 1]
        o_re, o_im = sandwich(
            table_of(s), w_re * p_re - w_im * p_im, w_re * p_im + w_im * p_re
        )
        psi[s + 1, 0] = o_re
        psi[s + 1, 1] = o_im
        return carry

    lax.fori_loop(0, layers, go_forward, 0)

    @pl.when(s_me < last)
    def _():
        wave_copy().start()
        adj_copy().wait_recv()

    @pl.when(s_me == last)
    def _():
        f_re, f_im = psi[layers, 0], psi[layers, 1]
        residual = f_re * f_re + f_im * f_im - meas[...]
        adj[layers, 0] = residual * f_re
        adj[layers, 1] = residual * f_im

    def go_back(step, carry):
        s = layers - 1 - step
        i_re, minus_im = sandwich(table_of(s), adj[s + 1, 0], -adj[s + 1, 1])
        i_im = -minus_im
        w_re, w_im = win[s, 0], win[s, 1]
        adj[s, 0] = w_re * i_re + w_im * i_im
        adj[s, 1] = w_re * i_im - w_im * i_re

        @pl.when((s == 0) & (s_me > 0))
        def _():
            adj_copy().start()

        p_re, p_im = psi[s, 0], psi[s, 1]
        terms = (p_re * i_re + p_im * i_im, p_re * i_im - p_im * i_re)
        for side in range(2):
            cols = own_cols(side)
            for part in range(2):
                here = terms[part][:, sides[side]]
                gzs[s, side, part] = jnp.where(cols, 0.0, here)
                term[s, part, :, sides[side]] = jnp.where(cols, here, 0.0)
        for copy in gz_copies(s):
            copy.start()
        return carry

    lax.fori_loop(0, layers, go_back, 0)

    def send_rows(step, carry):
        s = layers - 1 - step
        for copy in gz_copies(s):
            copy.wait_recv()
        rows = my_rows()
        for side in range(2):
            theirs = their_rows(side)
            for part in range(2):
                mine = term[s, part, :, sides[side]]
                came = gzr[s, side, part]
                gys[s, part, :, sides[side]] = jnp.where(rows, 0.0, mine) + jnp.where(
                    theirs, 0.0, came
                )
                term[s, part, :, sides[side]] = jnp.where(rows, mine, 0.0) + jnp.where(
                    theirs, came, 0.0
                )
        for copy in gy_copies(s):
            copy.start()
        return carry

    lax.fori_loop(0, layers, send_rows, 0)

    def finish(step, carry):
        s = layers - 1 - step
        for copy in gy_copies(s):
            copy.wait_recv()
        out[s] = obj[s] - STEP_SIZE * (term[s] + gyr[s])
        return carry

    lax.fori_loop(0, layers, finish, 0)

    for copy in pos_copies():
        copy.wait_send()
    for s in range(layers):
        for copies in (y_copies, z_copies, gz_copies, gy_copies):
            for copy in copies(s):
                copy.wait_send()

    @pl.when(s_me < last)
    def _():
        wave_copy().wait_send()

    @pl.when(s_me > 0)
    def _():
        adj_copy().wait_send()


def body(object_field, illumination, positions, measured):
    layers = object_field.shape[0]
    width = illumination.shape[-1]
    half = width // 2
    counts = tuple(lax.axis_size(a) for a in ("tx", "ty", "sl"))
    offset = positions.reshape(2)
    rolled = jnp.roll(illumination, (offset[0] - half, offset[1] - half), axis=(1, 2))
    pos = jnp.broadcast_to(offset[:, None, None], (2, 8, half)).astype(jnp.int32)
    tables = jnp.asarray(build_tables(width))
    f32 = jnp.float32
    wave = (layers, 2, width, width)
    strips = (layers, 2, 2, width, half)
    pairs = pltpu.SemaphoreType.DMA((layers, 2))
    two = pltpu.SemaphoreType.DMA((2,))
    return pl.pallas_call(
        functools.partial(kernel, counts),
        out_shape=jax.ShapeDtypeStruct(object_field.shape, f32),
        in_specs=[pl.BlockSpec(memory_space=pltpu.VMEM)] * 5,
        out_specs=pl.BlockSpec(memory_space=pltpu.VMEM),
        scratch_shapes=[
            pltpu.VMEM((2, 2, 2 * width, 2 * width), jnp.bfloat16),
            pltpu.VMEM((2, 2, 2 * width, 2 * width), jnp.bfloat16),
            pltpu.VMEM(wave, f32),
            pltpu.VMEM(strips, f32),
            pltpu.VMEM(strips, f32),
            pltpu.VMEM(wave, f32),
            pltpu.VMEM((layers + 1, 2, width, width), f32),
            pltpu.VMEM((layers + 1, 2, width, width), f32),
            pltpu.VMEM(wave, f32),
            pltpu.VMEM(strips, f32),
            pltpu.VMEM(strips, f32),
            pltpu.VMEM(wave, f32),
            pltpu.VMEM(wave, f32),
            pltpu.VMEM((2, 2, 8, half), jnp.int32),
        ]
        + [pairs] * 8
        + [two] * 4,
        compiler_params=pltpu.CompilerParams(
            collective_id=0, has_side_effects=True, vmem_limit_bytes=48 * 1024 * 1024
        ),
    )(object_field, rolled, pos, measured.reshape(width, width), tables)


def solution(mesh):
    placed = (
        P("sl", None, "tx", "ty"),
        P(),
        P("tx", "ty", None, None),
        P("tx", "ty", None, None, None),
    )
    return jax.shard_map(
        body, mesh=mesh, in_specs=placed, out_specs=P("sl", None, "tx", "ty"), check_vma=False
    )
```

```python
import functools

import jax
import jax.numpy as jnp
import ml_dtypes
import numpy as np
from jax import lax
from jax.experimental import pallas as pl
from jax.experimental.pallas import tpu as pltpu
from jax.sharding import PartitionSpec as P

STEP_SIZE = 0.5
MESH = pl.DeviceIdType.MESH


def high_low(x):
    high = x.astype(np.float32).astype(ml_dtypes.bfloat16)
    low = (x - high.astype(np.float64)).astype(np.float32).astype(ml_dtypes.bfloat16)
    return high, low


def build_tables(length):
    k = np.arange(length)
    angles = (np.outer(k, k) % length) * (-2.0 * np.pi / length)
    forward = np.exp(1j * angles) / np.sqrt(length)
    q = np.where(k < length // 2, k, k - length)
    phases = np.exp(-1j * np.pi * (q * q % (4 * length)) / (2 * length))
    spread = (np.conj(forward) * phases[None, :]) @ forward
    both = []
    for matrix in (spread, forward):
        real_h, real_l = high_low(matrix.real)
        imag_h, imag_l = high_low(matrix.imag)
        both.append(np.stack([real_h, imag_h, real_l, imag_l]))
    return np.stack(both)


def split(x):
    high = x.astype(jnp.bfloat16)
    low = (x - high.astype(jnp.float32)).astype(jnp.bfloat16)
    return high, low


def dot(a, b):
    return jnp.dot(a, b, preferred_element_type=jnp.float32)


def kernel(
    counts,
    obj,
    ill,
    pos,
    meas,
    tab,
    out,
    t_left,
    t_right,
    ybuf,
    zs,
    zr,
    win,
    psi,
    adj,
    term,
    gzs,
    gzr,
    gys,
    gyr,
    posbuf,
    y_s,
    y_r,
    z_s,
    z_r,
    gz_s,
    gz_r,
    gy_s,
    gy_r,
    p_s,
    p_r,
    w_s,
    w_r,
):
    nx, ny, ns = counts
    layers = obj.shape[0]
    width = obj.shape[-1]
    half = width // 2
    x = lax.axis_index("tx")
    y = lax.axis_index("ty")
    s_me = lax.axis_index("sl")
    last = ns - 1
    up = (lax.rem(x + nx - 1, nx), y, s_me)
    down = (lax.rem(x + 1, nx), y, s_me)
    left = (x, lax.rem(y + ny - 1, ny), s_me)
    right = (x, lax.rem(y + 1, ny), s_me)
    after = (x, y, jnp.minimum(s_me + 1, last))
    before = (x, y, jnp.maximum(s_me - 1, 0))
    top, bottom = pl.ds(0, half), pl.ds(half, half)

    barrier = pltpu.get_barrier_semaphore()
    for there in (up, down, left, right):
        pl.semaphore_signal(barrier, inc=1, device_id=there, device_id_type=MESH)

    @pl.when(s_me > 0)
    def _():
        pl.semaphore_signal(barrier, inc=1, device_id=before, device_id_type=MESH)

    @pl.when(s_me < last)
    def _():
        pl.semaphore_signal(barrier, inc=1, device_id=after, device_id_type=MESH)

    ends = jnp.where(s_me > 0, 1, 0) + jnp.where(s_me < last, 1, 0)
    pl.semaphore_wait(barrier, 4 + ends)

    def remote(src, dst, send, recv, there):
        return pltpu.make_async_remote_copy(
            src_ref=src,
            dst_ref=dst,
            send_sem=send,
            recv_sem=recv,
            device_id=there,
            device_id_type=MESH,
        )

    def pos_copies():
        return [
            remote(pos, posbuf.at[0], p_s.at[0], p_r.at[0], right),
            remote(pos, posbuf.at[1], p_s.at[1], p_r.at[1], left),
        ]

    def y_copies(s, c):
        a, b = obj.at[s, c], ybuf.at[s, c]
        return [
            remote(a.at[top], b.at[top], y_s.at[s, c, 0], y_r.at[s, c, 0], up),
            remote(a.at[bottom], b.at[bottom], y_s.at[s, c, 1], y_r.at[s, c, 1], down),
        ]

    def z_copies(s, c):
        return [
            remote(zs.at[s, 0, c], zr.at[s, 0, c], z_s.at[s, c, 0], z_r.at[s, c, 0], left),
            remote(zs.at[s, 1, c], zr.at[s, 1, c], z_s.at[s, c, 1], z_r.at[s, c, 1], right),
        ]

    def gz_copies(s, c):
        return [
            remote(gzs.at[s, 0, c], gzr.at[s, 0, c], gz_s.at[s, c, 0], gz_r.at[s, c, 0], right),
            remote(gzs.at[s, 1, c], gzr.at[s, 1, c], gz_s.at[s, c, 1], gz_r.at[s, c, 1], left),
        ]

    def gy_copies(s, c):
        a, b = gys.at[s, c], gyr.at[s, c]
        return [
            remote(a.at[top], b.at[top], gy_s.at[s, c, 0], gy_r.at[s, c, 0], down),
            remote(a.at[bottom], b.at[bottom], gy_s.at[s, c, 1], gy_r.at[s, c, 1], up),
        ]

    def wave_copy():
        return remote(psi.at[layers], psi.at[0], w_s.at[0], w_r.at[0], after)

    def adj_copy():
        return remote(adj.at[0], adj.at[layers], w_s.at[1], w_r.at[1], before)

    for copy in pos_copies():
        copy.start()
    for s in range(layers):
        for c in range(2):
            for copy in y_copies(s, c):
                copy.start()

    for which in range(2):
        for part in range(2):
            real = tab[which, 2 * part]
            imag = tab[which, 2 * part + 1]
            t_right[which, part, 0:width, 0:width] = real
            t_right[which, part, 0:width, width : 2 * width] = imag
            t_right[which, part, width : 2 * width, 0:width] = -imag
            t_right[which, part, width : 2 * width, width : 2 * width] = real
            first = slice(2 * part * width, (2 * part + 1) * width)
            second = slice((2 * part + 1) * width, (2 * part + 2) * width)
            t_left[which, first, 0:width] = real
            t_left[which, first, width : 2 * width] = -imag
            t_left[which, second, 0:width] = imag
            t_left[which, second, width : 2 * width] = real

    @pl.when(s_me == 0)
    def _():
        psi[0] = ill[...]

    def own_rows(row):
        cells = lax.broadcasted_iota(jnp.int32, (width, half), 0)
        return (cells >= row - half) & (cells < row + half)

    def own_cols(side):
        cells = lax.broadcasted_iota(jnp.int32, (width, half), 1) + side * half
        col = pos[1, 0:1, 0:half]
        return (cells >= col - half) & (cells < col + half)

    def my_rows():
        return own_rows(pos[0, 0:1, 0:half])

    def their_rows(slot):
        return own_rows(posbuf[slot, 0, 0:1, 0:half])

    sides = (slice(0, half), slice(half, width))

    for copy in pos_copies():
        copy.wait_recv()

    def send_columns(s, carry):
        for part in range(2):
            for copy in y_copies(s, part):
                copy.wait_recv()
            for side in range(2):
                zs[s, side, part] = jnp.where(
                    their_rows(side),
                    obj[s, part, :, sides[side]],
                    ybuf[s, part, :, sides[side]],
                )
            for copy in z_copies(s, part):
                copy.start()
        return carry

    lax.fori_loop(0, layers, send_columns, 0)

    def sandwich(which, real, imag):
        wide = 2 * width
        high, low = split(jnp.concatenate([real, imag], axis=0))
        two = dot(t_left[which], high)
        done = two[:wide] + two[wide:] + dot(t_left[which, 0:wide], low)
        high, low = split(jnp.concatenate([done[:width], done[width:]], axis=1))
        two = dot(jnp.concatenate([high, low], axis=0), t_right[which, 0])
        done = two[:width] + two[width:] + dot(high, t_right[which, 1])
        return done[:, :width], done[:, width:]

    def table_of(s):
        return jnp.where((s_me == last) & (s == layers - 1), 1, 0)

    def go_forward(s, carry):
        for c in range(2):
            for copy in z_copies(s, c):
                copy.wait_recv()
        rows = my_rows()
        for side in range(2):
            cols = own_cols(side)
            for part in range(2):
                mixed = jnp.where(
                    rows, obj[s, part, :, sides[side]], ybuf[s, part, :, sides[side]]
                )
                win[s, part, :, sides[side]] = jnp.where(cols, mixed, zr[s, side, part])

        @pl.when((s == 0) & (s_me > 0))
        def _():
            wave_copy().wait_recv()

        w_re, w_im = win[s, 0], win[s, 1]
        p_re, p_im = psi[s, 0], psi[s, 1]
        o_re, o_im = sandwich(
            table_of(s), w_re * p_re - w_im * p_im, w_re * p_im + w_im * p_re
        )
        psi[s + 1, 0] = o_re
        psi[s + 1, 1] = o_im
        return carry

    lax.fori_loop(0, layers, go_forward, 0)

    @pl.when(s_me < last)
    def _():
        wave_copy().start()
        adj_copy().wait_recv()

    @pl.when(s_me == last)
    def _():
        f_re, f_im = psi[layers, 0], psi[layers, 1]
        residual = f_re * f_re + f_im * f_im - meas[...]
        adj[layers, 0] = residual * f_re
        adj[layers, 1] = residual * f_im

    def go_back(step, carry):
        s = layers - 1 - step
        i_re, minus_im = sandwich(table_of(s), adj[s + 1, 0], -adj[s + 1, 1])
        i_im = -minus_im
        w_re, w_im = win[s, 0], win[s, 1]
        adj[s, 0] = w_re * i_re + w_im * i_im
        adj[s, 1] = w_re * i_im - w_im * i_re

        @pl.when((s == 0) & (s_me > 0))
        def _():
            adj_copy().start()

        p_re, p_im = psi[s, 0], psi[s, 1]
        terms = (p_re * i_re + p_im * i_im, p_re * i_im - p_im * i_re)
        for part in range(2):
            for side in range(2):
                cols = own_cols(side)
                here = terms[part][:, sides[side]]
                gzs[s, side, part] = jnp.where(cols, 0.0, here)
                term[s, part, :, sides[side]] = jnp.where(cols, here, 0.0)
            for copy in gz_copies(s, part):
                copy.start()
        return carry

    lax.fori_loop(0, layers, go_back, 0)

    def send_rows(step, carry):
        s = layers - 1 - step
        for part in range(2):
            for copy in gz_copies(s, part):
                copy.wait_recv()
            rows = my_rows()
            for side in range(2):
                theirs = their_rows(side)
                mine = term[s, part, :, sides[side]]
                came = gzr[s, side, part]
                gys[s, part, :, sides[side]] = jnp.where(rows, 0.0, mine) + jnp.where(
                    theirs, 0.0, came
                )
                term[s, part, :, sides[side]] = jnp.where(rows, mine, 0.0) + jnp.where(
                    theirs, came, 0.0
                )
            for copy in gy_copies(s, part):
                copy.start()
        return carry

    lax.fori_loop(0, layers, send_rows, 0)

    def finish(step, carry):
        s = layers - 1 - step
        for c in range(2):
            for copy in gy_copies(s, c):
                copy.wait_recv()
            out[s, c] = obj[s, c] - STEP_SIZE * (term[s, c] + gyr[s, c])
        return carry

    lax.fori_loop(0, layers, finish, 0)

    for copy in pos_copies():
        copy.wait_send()
    for s in range(layers):
        for copies in (y_copies, z_copies, gz_copies, gy_copies):
            for copy in copies(s, 0) + copies(s, 1):
                copy.wait_send()

    @pl.when(s_me < last)
    def _():
        wave_copy().wait_send()

    @pl.when(s_me > 0)
    def _():
        adj_copy().wait_send()


def body(object_field, illumination, positions, measured):
    layers = object_field.shape[0]
    width = illumination.shape[-1]
    half = width // 2
    counts = tuple(lax.axis_size(a) for a in ("tx", "ty", "sl"))
    offset = positions.reshape(2)
    rolled = jnp.roll(illumination, (offset[0] - half, offset[1] - half), axis=(1, 2))
    pos = jnp.broadcast_to(offset[:, None, None], (2, 8, half)).astype(jnp.int32)
    tables = jnp.asarray(build_tables(width))
    f32 = jnp.float32
    wave = (layers, 2, width, width)
    strips = (layers, 2, 2, width, half)
    pairs = pltpu.SemaphoreType.DMA((layers, 2, 2))
    two = pltpu.SemaphoreType.DMA((2,))
    return pl.pallas_call(
        functools.partial(kernel, counts),
        out_shape=jax.ShapeDtypeStruct(object_field.shape, f32),
        in_specs=[pl.BlockSpec(memory_space=pltpu.VMEM)] * 5,
        out_specs=pl.BlockSpec(memory_space=pltpu.VMEM),
        scratch_shapes=[
            pltpu.VMEM((2, 4 * width, 2 * width), jnp.bfloat16),
            pltpu.VMEM((2, 2, 2 * width, 2 * width), jnp.bfloat16),
            pltpu.VMEM(wave, f32),
            pltpu.VMEM(strips, f32),
            pltpu.VMEM(strips, f32),
            pltpu.VMEM(wave, f32),
            pltpu.VMEM((layers + 1, 2, width, width), f32),
            pltpu.VMEM((layers + 1, 2, width, width), f32),
            pltpu.VMEM(wave, f32),
            pltpu.VMEM(strips, f32),
            pltpu.VMEM(strips, f32),
            pltpu.VMEM(wave, f32),
            pltpu.VMEM(wave, f32),
            pltpu.VMEM((2, 2, 8, half), jnp.int32),
        ]
        + [pairs] * 8
        + [two] * 4,
        compiler_params=pltpu.CompilerParams(
            collective_id=0, has_side_effects=True, vmem_limit_bytes=48 * 1024 * 1024
        ),
    )(object_field, rolled, pos, measured.reshape(width, width), tables)


def solution(mesh):
    placed = (
        P("sl", None, "tx", "ty"),
        P(),
        P("tx", "ty", None, None),
        P("tx", "ty", None, None, None),
    )
    return jax.shard_map(
        body, mesh=mesh, in_specs=placed, out_specs=P("sl", None, "tx", "ty"), check_vma=False
    )
```

```python
import functools

import jax
import jax.numpy as jnp
import ml_dtypes
import numpy as np
from jax import lax
from jax.experimental import pallas as pl
from jax.experimental.pallas import tpu as pltpu
from jax.sharding import PartitionSpec as P

STEP_SIZE = 0.5
MESH = pl.DeviceIdType.MESH


def high_low(x):
    high = x.astype(np.float32).astype(ml_dtypes.bfloat16)
    low = (x - high.astype(np.float64)).astype(np.float32).astype(ml_dtypes.bfloat16)
    return high, low


def build_tables(length):
    k = np.arange(length)
    angles = (np.outer(k, k) % length) * (-2.0 * np.pi / length)
    forward = np.exp(1j * angles) / np.sqrt(length)
    q = np.where(k < length // 2, k, k - length)
    phases = np.exp(-1j * np.pi * (q * q % (4 * length)) / (2 * length))
    spread = (np.conj(forward) * phases[None, :]) @ forward
    both = []
    for matrix in (spread, forward):
        real_h, real_l = high_low(matrix.real)
        imag_h, imag_l = high_low(matrix.imag)
        both.append(np.stack([real_h, imag_h, real_l, imag_l]))
    return np.stack(both)


def split(x):
    high = x.astype(jnp.bfloat16)
    low = (x - high.astype(jnp.float32)).astype(jnp.bfloat16)
    return high, low


def dot(a, b):
    return jnp.dot(a, b, preferred_element_type=jnp.float32)


def kernel(
    counts,
    obj,
    ill,
    pos,
    meas,
    tab,
    out,
    t_left,
    t_right,
    ybuf,
    zs,
    zr,
    win,
    psi,
    adj,
    term,
    gzs,
    gzr,
    gys,
    gyr,
    posbuf,
    y_s,
    y_r,
    z_s,
    z_r,
    gz_s,
    gz_r,
    gy_s,
    gy_r,
    p_s,
    p_r,
    x_s,
    x_r,
    m_s,
    m_r,
    n_s,
    n_r,
):
    nx, ny, ns = counts
    layers = obj.shape[0]
    width = obj.shape[-1]
    half = width // 2
    x = lax.axis_index("tx")
    y = lax.axis_index("ty")
    s_me = lax.axis_index("sl")
    last = ns - 1
    up = (lax.rem(x + nx - 1, nx), y, s_me)
    down = (lax.rem(x + 1, nx), y, s_me)
    left = (x, lax.rem(y + ny - 1, ny), s_me)
    right = (x, lax.rem(y + 1, ny), s_me)
    pair, core = lax.div(s_me, 2), lax.rem(s_me, 2)
    last_pair = ns // 2 - 1
    depth = 2 * layers
    mate = (x, y, s_me + 1 - 2 * core)
    after = (x, y, jnp.minimum(s_me + 2, last))
    before = (x, y, jnp.maximum(s_me - 2, 0))
    my_half = pl.ds(pl.multiple_of(core * half, half), half)
    top, bottom = pl.ds(0, half), pl.ds(half, half)

    barrier = pltpu.get_barrier_semaphore()
    for there in (up, down, left, right, mate):
        pl.semaphore_signal(barrier, inc=1, device_id=there, device_id_type=MESH)

    @pl.when(pair > 0)
    def _():
        pl.semaphore_signal(barrier, inc=1, device_id=before, device_id_type=MESH)

    @pl.when(pair < last_pair)
    def _():
        pl.semaphore_signal(barrier, inc=1, device_id=after, device_id_type=MESH)

    ends = jnp.where(pair > 0, 1, 0) + jnp.where(pair < last_pair, 1, 0)
    pl.semaphore_wait(barrier, 5 + ends)

    def remote(src, dst, send, recv, there):
        return pltpu.make_async_remote_copy(
            src_ref=src,
            dst_ref=dst,
            send_sem=send,
            recv_sem=recv,
            device_id=there,
            device_id_type=MESH,
        )

    def pos_copies():
        return [
            remote(pos, posbuf.at[0], p_s.at[0], p_r.at[0], right),
            remote(pos, posbuf.at[1], p_s.at[1], p_r.at[1], left),
        ]

    def y_copies(s, c):
        a, b = obj.at[s, c], ybuf.at[s, c]
        return [
            remote(a.at[top], b.at[top], y_s.at[s, c, 0], y_r.at[s, c, 0], up),
            remote(a.at[bottom], b.at[bottom], y_s.at[s, c, 1], y_r.at[s, c, 1], down),
        ]

    def z_copies(s, c):
        return [
            remote(zs.at[s, 0, c], zr.at[s, 0, c], z_s.at[s, c, 0], z_r.at[s, c, 0], left),
            remote(zs.at[s, 1, c], zr.at[s, 1, c], z_s.at[s, c, 1], z_r.at[s, c, 1], right),
        ]

    def gz_copies(s, c):
        return [
            remote(gzs.at[s, 0, c], gzr.at[s, 0, c], gz_s.at[s, c, 0], gz_r.at[s, c, 0], right),
            remote(gzs.at[s, 1, c], gzr.at[s, 1, c], gz_s.at[s, c, 1], gz_r.at[s, c, 1], left),
        ]

    def gy_copies(s, c):
        a, b = gys.at[s, c], gyr.at[s, c]
        return [
            remote(a.at[top], b.at[top], gy_s.at[s, c, 0], gy_r.at[s, c, 0], down),
            remote(a.at[bottom], b.at[bottom], gy_s.at[s, c, 1], gy_r.at[s, c, 1], up),
        ]

    def window_copy(s):
        at = core * layers + s
        return remote(win.at[at], win.at[at], n_s.at[s], n_r.at[s], mate)

    def wave_copy(c):
        src, dst = psi.at[depth, c, my_half], psi.at[0, c, my_half]
        return remote(src, dst, x_s.at[0, c], x_r.at[0, c], after)

    def wave_share(c):
        block = psi.at[0, c, my_half]
        return remote(block, block, m_s.at[0, c], m_r.at[0, c], mate)

    def adj_copy(c):
        src, dst = adj.at[0, c, my_half], adj.at[depth, c, my_half]
        return remote(src, dst, x_s.at[1, c], x_r.at[1, c], before)

    def adj_share(c):
        block = adj.at[depth, c, my_half]
        return remote(block, block, m_s.at[1, c], m_r.at[1, c], mate)

    def receive(copy, share):
        for c in range(2):
            copy(c).wait_recv()
            share(c).start()
        for c in range(2):
            share(c).wait_recv()

    for copy in pos_copies():
        copy.start()
    for s in range(layers):
        for c in range(2):
            for copy in y_copies(s, c):
                copy.start()

    for which in range(2):
        for part in range(2):
            real = tab[which, 2 * part]
            imag = tab[which, 2 * part + 1]
            t_right[which, part, 0:width, 0:width] = real
            t_right[which, part, 0:width, width : 2 * width] = imag
            t_right[which, part, width : 2 * width, 0:width] = -imag
            t_right[which, part, width : 2 * width, width : 2 * width] = real
            first = slice(2 * part * width, (2 * part + 1) * width)
            second = slice((2 * part + 1) * width, (2 * part + 2) * width)
            t_left[which, first, 0:width] = real
            t_left[which, first, width : 2 * width] = -imag
            t_left[which, second, 0:width] = imag
            t_left[which, second, width : 2 * width] = real

    @pl.when(pair == 0)
    def _():
        psi[0] = ill[...]

    def own_rows(row):
        cells = lax.broadcasted_iota(jnp.int32, (width, half), 0)
        return (cells >= row - half) & (cells < row + half)

    def own_cols(side):
        cells = lax.broadcasted_iota(jnp.int32, (width, half), 1) + side * half
        col = pos[1, 0:1, 0:half]
        return (cells >= col - half) & (cells < col + half)

    def my_rows():
        return own_rows(pos[0, 0:1, 0:half])

    def their_rows(slot):
        return own_rows(posbuf[slot, 0, 0:1, 0:half])

    sides = (slice(0, half), slice(half, width))

    for copy in pos_copies():
        copy.wait_recv()

    def send_columns(s, carry):
        for part in range(2):
            for copy in y_copies(s, part):
                copy.wait_recv()
            for side in range(2):
                zs[s, side, part] = jnp.where(
                    their_rows(side),
                    obj[s, part, :, sides[side]],
                    ybuf[s, part, :, sides[side]],
                )
            for copy in z_copies(s, part):
                copy.start()
        return carry

    lax.fori_loop(0, layers, send_columns, 0)

    def sandwich(which, real, imag):
        wide = 2 * width
        high, low = split(jnp.concatenate([real, imag], axis=0))
        two = dot(t_left[which], high)
        done = two[:wide] + two[wide:] + dot(t_left[which, 0:wide], low)
        high, low = split(jnp.concatenate([done[:width], done[width:]], axis=1))
        two = dot(jnp.concatenate([high, low], axis=0), t_right[which, 0])
        done = two[:width] + two[width:] + dot(high, t_right[which, 1])
        return done[:, :width], done[:, width:]

    def table_of(g):
        return jnp.where((pair == last_pair) & (g == depth - 1), 1, 0)

    def go_forward(g, carry):
        owner = lax.div(g, layers)

        @pl.when(owner != core)
        def _():
            window_copy(g - owner * layers).wait_recv()

        w_re, w_im = win[g, 0], win[g, 1]
        p_re, p_im = psi[g, 0], psi[g, 1]
        o_re, o_im = sandwich(
            table_of(g), w_re * p_re - w_im * p_im, w_re * p_im + w_im * p_re
        )
        psi[g + 1, 0] = o_re
        psi[g + 1, 1] = o_im
        return carry

    def build_window(s, carry):
        for c in range(2):
            for copy in z_copies(s, c):
                copy.wait_recv()
        rows = my_rows()
        at = core * layers + s
        for side in range(2):
            cols = own_cols(side)
            for part in range(2):
                mixed = jnp.where(
                    rows, obj[s, part, :, sides[side]], ybuf[s, part, :, sides[side]]
                )
                win[at, part, :, sides[side]] = jnp.where(cols, mixed, zr[s, side, part])
        window_copy(s).start()

        @pl.when(pair == 0)
        def _():
            go_forward(s, 0)

        return carry

    lax.fori_loop(0, layers, build_window, 0)

    @pl.when(pair > 0)
    def _():
        receive(wave_copy, wave_share)

    lax.fori_loop(jnp.where(pair == 0, layers, 0), depth, go_forward, 0)

    @pl.when(pair < last_pair)
    def _():
        for c in range(2):
            wave_copy(c).start()
        receive(adj_copy, adj_share)

    @pl.when(pair == last_pair)
    def _():
        f_re, f_im = psi[depth, 0], psi[depth, 1]
        residual = f_re * f_re + f_im * f_im - meas[...]
        adj[depth, 0] = residual * f_re
        adj[depth, 1] = residual * f_im

    def go_back(step, carry):
        g = depth - 1 - step
        i_re, minus_im = sandwich(table_of(g), adj[g + 1, 0], -adj[g + 1, 1])
        i_im = -minus_im
        w_re, w_im = win[g, 0], win[g, 1]
        adj[g, 0] = w_re * i_re + w_im * i_im
        adj[g, 1] = w_re * i_im - w_im * i_re

        @pl.when((g == 0) & (pair > 0))
        def _():
            for c in range(2):
                adj_copy(c).start()

        @pl.when(lax.div(g, layers) == core)
        def _():
            s = g - core * layers
            p_re, p_im = psi[g, 0], psi[g, 1]
            terms = (p_re * i_re + p_im * i_im, p_re * i_im - p_im * i_re)
            for part in range(2):
                for side in range(2):
                    cols = own_cols(side)
                    here = terms[part][:, sides[side]]
                    gzs[s, side, part] = jnp.where(cols, 0.0, here)
                    term[s, part, :, sides[side]] = jnp.where(cols, here, 0.0)
                for copy in gz_copies(s, part):
                    copy.start()

        return carry

    lax.fori_loop(0, jnp.where((pair == 0) & (core == 1), layers, depth), go_back, 0)

    def send_rows(step, carry):
        s = layers - 1 - step
        for part in range(2):
            for copy in gz_copies(s, part):
                copy.wait_recv()
            rows = my_rows()
            for side in range(2):
                theirs = their_rows(side)
                mine = term[s, part, :, sides[side]]
                came = gzr[s, side, part]
                gys[s, part, :, sides[side]] = jnp.where(rows, 0.0, mine) + jnp.where(
                    theirs, 0.0, came
                )
                term[s, part, :, sides[side]] = jnp.where(rows, mine, 0.0) + jnp.where(
                    theirs, came, 0.0
                )
            for copy in gy_copies(s, part):
                copy.start()
        return carry

    lax.fori_loop(0, layers, send_rows, 0)

    def finish(step, carry):
        s = layers - 1 - step
        for c in range(2):
            for copy in gy_copies(s, c):
                copy.wait_recv()
            out[s, c] = obj[s, c] - STEP_SIZE * (term[s, c] + gyr[s, c])
        return carry

    lax.fori_loop(0, layers, finish, 0)

    for copy in pos_copies():
        copy.wait_send()
    for s in range(layers):
        for copies in (y_copies, z_copies, gz_copies, gy_copies):
            for copy in copies(s, 0) + copies(s, 1):
                copy.wait_send()

        window_copy(s).wait_send()

    @pl.when(pair < last_pair)
    def _():
        for c in range(2):
            wave_copy(c).wait_send()
            adj_share(c).wait_send()

    @pl.when(pair > 0)
    def _():
        for c in range(2):
            adj_copy(c).wait_send()
            wave_share(c).wait_send()


def body(object_field, illumination, positions, measured):
    layers = object_field.shape[0]
    width = illumination.shape[-1]
    half = width // 2
    counts = tuple(lax.axis_size(a) for a in ("tx", "ty", "sl"))
    offset = positions.reshape(2)
    rolled = jnp.roll(illumination, (offset[0] - half, offset[1] - half), axis=(1, 2))
    pos = jnp.broadcast_to(offset[:, None, None], (2, 8, half)).astype(jnp.int32)
    tables = jnp.asarray(build_tables(width))
    f32 = jnp.float32
    wave = (layers, 2, width, width)
    strips = (layers, 2, 2, width, half)
    pairs = pltpu.SemaphoreType.DMA((layers, 2, 2))
    two = pltpu.SemaphoreType.DMA((2,))
    square = pltpu.SemaphoreType.DMA((2, 2))
    windows = pltpu.SemaphoreType.DMA((layers,))
    return pl.pallas_call(
        functools.partial(kernel, counts),
        out_shape=jax.ShapeDtypeStruct(object_field.shape, f32),
        in_specs=[pl.BlockSpec(memory_space=pltpu.VMEM)] * 5,
        out_specs=pl.BlockSpec(memory_space=pltpu.VMEM),
        scratch_shapes=[
            pltpu.VMEM((2, 4 * width, 2 * width), jnp.bfloat16),
            pltpu.VMEM((2, 2, 2 * width, 2 * width), jnp.bfloat16),
            pltpu.VMEM(wave, f32),
            pltpu.VMEM(strips, f32),
            pltpu.VMEM(strips, f32),
            pltpu.VMEM((2 * layers, 2, width, width), f32),
            pltpu.VMEM((2 * layers + 1, 2, width, width), f32),
            pltpu.VMEM((2 * layers + 1, 2, width, width), f32),
            pltpu.VMEM(wave, f32),
            pltpu.VMEM(strips, f32),
            pltpu.VMEM(strips, f32),
            pltpu.VMEM(wave, f32),
            pltpu.VMEM(wave, f32),
            pltpu.VMEM((2, 2, 8, half), jnp.int32),
        ]
        + [pairs] * 8
        + [two] * 2
        + [square] * 4
        + [windows] * 2,
        compiler_params=pltpu.CompilerParams(
            collective_id=0, has_side_effects=True, vmem_limit_bytes=48 * 1024 * 1024
        ),
    )(object_field, rolled, pos, measured.reshape(width, width), tables)


def solution(mesh):
    placed = (
        P("sl", None, "tx", "ty"),
        P(),
        P("tx", "ty", None, None),
        P("tx", "ty", None, None, None),
    )
    return jax.shard_map(
        body, mesh=mesh, in_specs=placed, out_specs=P("sl", None, "tx", "ty"), check_vma=False
    )
```

```python
import functools

import jax
import jax.numpy as jnp
import ml_dtypes
import numpy as np
from jax import lax
from jax.experimental import pallas as pl
from jax.experimental.pallas import tpu as pltpu
from jax.sharding import PartitionSpec as P

STEP_SIZE = 0.5
MESH = pl.DeviceIdType.MESH


def high_low(x):
    high = x.astype(np.float32).astype(ml_dtypes.bfloat16)
    low = (x - high.astype(np.float64)).astype(np.float32).astype(ml_dtypes.bfloat16)
    return high, low


def build_tables(length):
    k = np.arange(length)
    angles = (np.outer(k, k) % length) * (-2.0 * np.pi / length)
    forward = np.exp(1j * angles) / np.sqrt(length)
    q = np.where(k < length // 2, k, k - length)
    phases = np.exp(-1j * np.pi * (q * q % (4 * length)) / (2 * length))
    spread = (np.conj(forward) * phases[None, :]) @ forward
    both = []
    for matrix in (spread, forward):
        real_h, real_l = high_low(matrix.real)
        imag_h, imag_l = high_low(matrix.imag)
        both.append(np.stack([real_h, imag_h, real_l, imag_l]))
    return np.stack(both)


def split(x):
    high = x.astype(jnp.bfloat16)
    low = (x - high.astype(jnp.float32)).astype(jnp.bfloat16)
    return high, low


def dot(a, b):
    return jnp.dot(a, b, preferred_element_type=jnp.float32)


def kernel(
    counts,
    obj_in,
    ill,
    pos,
    meas,
    tab_in,
    out,
    obj,
    tab,
    t_left,
    t_right,
    ybuf,
    zs,
    zr,
    win,
    psi,
    adj,
    term,
    gzs,
    gzr,
    gys,
    gyr,
    posbuf,
    y_s,
    y_r,
    z_s,
    z_r,
    gz_s,
    gz_r,
    gy_s,
    gy_r,
    p_s,
    p_r,
    x_s,
    x_r,
    m_s,
    m_r,
    n_s,
    n_r,
    here_s,
):
    nx, ny, ns = counts
    obj_copy = pltpu.make_async_copy(obj_in, obj, here_s.at[0])
    tab_copy = pltpu.make_async_copy(tab_in, tab, here_s.at[1])
    obj_copy.start()
    tab_copy.start()
    layers = obj.shape[0]
    width = obj.shape[-1]
    half = width // 2
    x = lax.axis_index("tx")
    y = lax.axis_index("ty")
    s_me = lax.axis_index("sl")
    last = ns - 1
    up = (lax.rem(x + nx - 1, nx), y, s_me)
    down = (lax.rem(x + 1, nx), y, s_me)
    left = (x, lax.rem(y + ny - 1, ny), s_me)
    right = (x, lax.rem(y + 1, ny), s_me)
    pair, core = lax.div(s_me, 2), lax.rem(s_me, 2)
    last_pair = ns // 2 - 1
    depth = 2 * layers
    mate = (x, y, s_me + 1 - 2 * core)
    after = (x, y, jnp.minimum(s_me + 2, last))
    before = (x, y, jnp.maximum(s_me - 2, 0))
    my_half = pl.ds(pl.multiple_of(core * half, half), half)
    top, bottom = pl.ds(0, half), pl.ds(half, half)

    barrier = pltpu.get_barrier_semaphore()
    for there in (up, down, left, right, mate):
        pl.semaphore_signal(barrier, inc=1, device_id=there, device_id_type=MESH)

    @pl.when(pair > 0)
    def _():
        pl.semaphore_signal(barrier, inc=1, device_id=before, device_id_type=MESH)

    @pl.when(pair < last_pair)
    def _():
        pl.semaphore_signal(barrier, inc=1, device_id=after, device_id_type=MESH)

    ends = jnp.where(pair > 0, 1, 0) + jnp.where(pair < last_pair, 1, 0)
    pl.semaphore_wait(barrier, 5 + ends)

    def remote(src, dst, send, recv, there):
        return pltpu.make_async_remote_copy(
            src_ref=src,
            dst_ref=dst,
            send_sem=send,
            recv_sem=recv,
            device_id=there,
            device_id_type=MESH,
        )

    def pos_copies():
        return [
            remote(pos, posbuf.at[0], p_s.at[0], p_r.at[0], right),
            remote(pos, posbuf.at[1], p_s.at[1], p_r.at[1], left),
        ]

    def y_copies(s, c):
        a, b = obj_in.at[s, c], ybuf.at[s, c]
        return [
            remote(a.at[top], b.at[top], y_s.at[s, c, 0], y_r.at[s, c, 0], up),
            remote(a.at[bottom], b.at[bottom], y_s.at[s, c, 1], y_r.at[s, c, 1], down),
        ]

    def z_copies(s, c, h):
        rows = (top, bottom)[h]
        return [
            remote(
                zs.at[s, side, c, rows],
                zr.at[s, side, c, rows],
                z_s.at[s, c, h, side],
                z_r.at[s, c, h, side],
                (left, right)[side],
            )
            for side in range(2)
        ]

    def gz_copies(s, c, h):
        rows = (top, bottom)[h]
        return [
            remote(
                gzs.at[s, side, c, rows],
                gzr.at[s, side, c, rows],
                gz_s.at[s, c, h, side],
                gz_r.at[s, c, h, side],
                (right, left)[side],
            )
            for side in range(2)
        ]

    def gy_copies(s, c):
        a, b = gys.at[s, c], gyr.at[s, c]
        return [
            remote(a.at[top], b.at[top], gy_s.at[s, c, 0], gy_r.at[s, c, 0], down),
            remote(a.at[bottom], b.at[bottom], gy_s.at[s, c, 1], gy_r.at[s, c, 1], up),
        ]

    def window_copy(s):
        at = core * layers + s
        return remote(win.at[at], win.at[at], n_s.at[s], n_r.at[s], mate)

    def wave_copy(c):
        src, dst = psi.at[depth, c, my_half], psi.at[0, c, my_half]
        return remote(src, dst, x_s.at[0, c], x_r.at[0, c], after)

    def wave_share(c):
        block = psi.at[0, c, my_half]
        return remote(block, block, m_s.at[0, c], m_r.at[0, c], mate)

    def adj_copy(c):
        src, dst = adj.at[0, c, my_half], adj.at[depth, c, my_half]
        return remote(src, dst, x_s.at[1, c], x_r.at[1, c], before)

    def adj_share(c):
        block = adj.at[depth, c, my_half]
        return remote(block, block, m_s.at[1, c], m_r.at[1, c], mate)

    def receive(copy, share):
        for c in range(2):
            copy(c).wait_recv()
            share(c).start()
        for c in range(2):
            share(c).wait_recv()

    for copy in pos_copies():
        copy.start()
    for s in range(layers):
        for c in range(2):
            for copy in y_copies(s, c):
                copy.start()

    tab_copy.wait()
    for which in range(2):
        for part in range(2):
            real = tab[which, 2 * part]
            imag = tab[which, 2 * part + 1]
            t_right[which, part, 0:width, 0:width] = real
            t_right[which, part, 0:width, width : 2 * width] = imag
            t_right[which, part, width : 2 * width, 0:width] = -imag
            t_right[which, part, width : 2 * width, width : 2 * width] = real
            first = slice(2 * part * width, (2 * part + 1) * width)
            second = slice((2 * part + 1) * width, (2 * part + 2) * width)
            t_left[which, first, 0:width] = real
            t_left[which, first, width : 2 * width] = -imag
            t_left[which, second, 0:width] = imag
            t_left[which, second, width : 2 * width] = real

    @pl.when(pair == 0)
    def _():
        i0 = lax.broadcasted_iota(jnp.int32, (width, width), 0)
        i1 = lax.broadcasted_iota(jnp.int32, (width, width), 1)
        row = pos[0, 0:1, 0:1]
        col = pos[1, 0:1, 0:1]
        place_r = jnp.where(((i1 + row + half) & (width - 1)) == i0, 1.0, 0.0)
        place_c = jnp.where(((i0 + col + half) & (width - 1)) == i1, 1.0, 0.0)
        place_r = place_r.astype(jnp.bfloat16)
        place_c = place_c.astype(jnp.bfloat16)

        def thirds(value):
            high, middle = split(value)
            rest = value - high.astype(jnp.float32) - middle.astype(jnp.float32)
            return high, middle, rest.astype(jnp.bfloat16)

        for part in range(2):
            high, middle, low = thirds(ill[part])
            value = dot(place_r, high) + dot(place_r, middle) + dot(place_r, low)
            high, middle, low = thirds(value)
            psi[0, part] = dot(high, place_c) + dot(middle, place_c) + dot(low, place_c)

    def own_rows(row, h):
        shape = (width if h is None else half, half)
        cells = lax.broadcasted_iota(jnp.int32, shape, 0) + (h or 0) * half
        return (cells >= row - half) & (cells < row + half)

    def own_cols(side):
        cells = lax.broadcasted_iota(jnp.int32, (width, half), 1) + side * half
        col = pos[1, 0:1, 0:half]
        return (cells >= col - half) & (cells < col + half)

    def my_rows(h=None):
        return own_rows(pos[0, 0:1, 0:half], h)

    def their_rows(slot, h):
        return own_rows(posbuf[slot, 0, 0:1, 0:half], h)

    sides = (slice(0, half), slice(half, width))

    for copy in pos_copies():
        copy.wait_recv()

    obj_copy.wait()

    def send_columns(s, carry):
        for part in range(2):
            for h in range(2):
                y_copies(s, part)[h].wait_recv()
                for side in range(2):
                    zs[s, side, part, sides[h]] = jnp.where(
                        their_rows(side, h),
                        obj[s, part, sides[h], sides[side]],
                        ybuf[s, part, sides[h], sides[side]],
                    )
                for copy in z_copies(s, part, h):
                    copy.start()
        return carry

    lax.fori_loop(0, layers, send_columns, 0)

    def sandwich(which, real, imag):
        wide = 2 * width
        high, low = split(jnp.concatenate([real, imag], axis=0))
        two = dot(t_left[which], high)
        done = two[:wide] + two[wide:] + dot(t_left[which, 0:wide], low)
        high, low = split(jnp.concatenate([done[:width], done[width:]], axis=1))
        two = dot(jnp.concatenate([high, low], axis=0), t_right[which, 0])
        done = two[:width] + two[width:] + dot(high, t_right[which, 1])
        return done[:, :width], done[:, width:]

    def table_of(g):
        return jnp.where((pair == last_pair) & (g == depth - 1), 1, 0)

    def go_forward(g, carry):
        owner = lax.div(g, layers)

        @pl.when(owner != core)
        def _():
            window_copy(g - owner * layers).wait_recv()

        w_re, w_im = win[g, 0], win[g, 1]
        p_re, p_im = psi[g, 0], psi[g, 1]
        o_re, o_im = sandwich(
            table_of(g), w_re * p_re - w_im * p_im, w_re * p_im + w_im * p_re
        )
        psi[g + 1, 0] = o_re
        psi[g + 1, 1] = o_im
        return carry

    def build_window(s, carry):
        for c in range(2):
            for copy in z_copies(s, c, 0) + z_copies(s, c, 1):
                copy.wait_recv()
        rows = my_rows()
        at = core * layers + s
        for side in range(2):
            cols = own_cols(side)
            for part in range(2):
                mixed = jnp.where(
                    rows, obj[s, part, :, sides[side]], ybuf[s, part, :, sides[side]]
                )
                win[at, part, :, sides[side]] = jnp.where(cols, mixed, zr[s, side, part])
        window_copy(s).start()

        @pl.when(pair == 0)
        def _():
            go_forward(s, 0)

        return carry

    lax.fori_loop(0, layers, build_window, 0)

    @pl.when(pair > 0)
    def _():
        receive(wave_copy, wave_share)

    lax.fori_loop(jnp.where(pair == 0, layers, 0), depth, go_forward, 0)

    @pl.when(pair < last_pair)
    def _():
        for c in range(2):
            wave_copy(c).start()
        receive(adj_copy, adj_share)

    @pl.when(pair == last_pair)
    def _():
        f_re, f_im = psi[depth, 0], psi[depth, 1]
        residual = f_re * f_re + f_im * f_im - meas[...]
        adj[depth, 0] = residual * f_re
        adj[depth, 1] = residual * f_im

    def go_back(step, carry):
        g = depth - 1 - step
        i_re, minus_im = sandwich(table_of(g), adj[g + 1, 0], -adj[g + 1, 1])
        i_im = -minus_im
        w_re, w_im = win[g, 0], win[g, 1]
        adj[g, 0] = w_re * i_re + w_im * i_im
        adj[g, 1] = w_re * i_im - w_im * i_re

        @pl.when((g == 0) & (pair > 0))
        def _():
            for c in range(2):
                adj_copy(c).start()

        @pl.when(lax.div(g, layers) == core)
        def _():
            s = g - core * layers
            p_re, p_im = psi[g, 0], psi[g, 1]
            terms = (p_re * i_re + p_im * i_im, p_re * i_im - p_im * i_re)
            for part in range(2):
                for side in range(2):
                    cols = own_cols(side)
                    here = terms[part][:, sides[side]]
                    gzs[s, side, part] = jnp.where(cols, 0.0, here)
                    term[s, part, :, sides[side]] = jnp.where(cols, here, 0.0)
                for copy in gz_copies(s, part, 0) + gz_copies(s, part, 1):
                    copy.start()

        return carry

    lax.fori_loop(0, jnp.where((pair == 0) & (core == 1), layers, depth), go_back, 0)

    def send_rows(step, carry):
        s = layers - 1 - step
        for part in range(2):
            for h in range(2):
                for copy in gz_copies(s, part, h):
                    copy.wait_recv()
                rows = my_rows(h)
                for side in range(2):
                    theirs = their_rows(side, h)
                    mine = term[s, part, sides[h], sides[side]]
                    came = gzr[s, side, part, sides[h]]
                    gys[s, part, sides[h], sides[side]] = jnp.where(
                        rows, 0.0, mine
                    ) + jnp.where(theirs, 0.0, came)
                    term[s, part, sides[h], sides[side]] = jnp.where(
                        rows, mine, 0.0
                    ) + jnp.where(theirs, came, 0.0)
                gy_copies(s, part)[h].start()
        return carry

    lax.fori_loop(0, layers, send_rows, 0)

    def finish(step, carry):
        s = layers - 1 - step
        for c in range(2):
            for copy in gy_copies(s, c):
                copy.wait_recv()
            out[s, c] = obj[s, c] - STEP_SIZE * (term[s, c] + gyr[s, c])
        return carry

    lax.fori_loop(0, layers, finish, 0)

    for copy in pos_copies():
        copy.wait_send()
    for s in range(layers):
        for c in range(2):
            for copy in y_copies(s, c) + gy_copies(s, c):
                copy.wait_send()
            for h in range(2):
                for copy in z_copies(s, c, h) + gz_copies(s, c, h):
                    copy.wait_send()

        window_copy(s).wait_send()

    @pl.when(pair < last_pair)
    def _():
        for c in range(2):
            wave_copy(c).wait_send()
            adj_share(c).wait_send()

    @pl.when(pair > 0)
    def _():
        for c in range(2):
            adj_copy(c).wait_send()
            wave_share(c).wait_send()


def body(object_field, illumination, positions, measured):
    layers = object_field.shape[0]
    width = illumination.shape[-1]
    half = width // 2
    counts = tuple(lax.axis_size(a) for a in ("tx", "ty", "sl"))
    offset = positions.reshape(2)
    pos = jnp.broadcast_to(offset[:, None, None], (2, 8, half)).astype(jnp.int32)
    tables = jnp.asarray(build_tables(width))
    f32 = jnp.float32
    wave = (layers, 2, width, width)
    strips = (layers, 2, 2, width, half)
    pairs = pltpu.SemaphoreType.DMA((layers, 2, 2))
    quads = pltpu.SemaphoreType.DMA((layers, 2, 2, 2))
    two = pltpu.SemaphoreType.DMA((2,))
    square = pltpu.SemaphoreType.DMA((2, 2))
    windows = pltpu.SemaphoreType.DMA((layers,))
    return pl.pallas_call(
        functools.partial(kernel, counts),
        out_shape=jax.ShapeDtypeStruct(object_field.shape, f32),
        in_specs=[pl.BlockSpec(memory_space=pl.ANY)]
        + [pl.BlockSpec(memory_space=pltpu.VMEM)] * 3
        + [pl.BlockSpec(memory_space=pl.ANY)],
        out_specs=pl.BlockSpec(memory_space=pltpu.VMEM),
        scratch_shapes=[
            pltpu.VMEM(wave, f32),
            pltpu.VMEM(tables.shape, jnp.bfloat16),
            pltpu.VMEM((2, 4 * width, 2 * width), jnp.bfloat16),
            pltpu.VMEM((2, 2, 2 * width, 2 * width), jnp.bfloat16),
            pltpu.VMEM(wave, f32),
            pltpu.VMEM(strips, f32),
            pltpu.VMEM(strips, f32),
            pltpu.VMEM((2 * layers, 2, width, width), f32),
            pltpu.VMEM((2 * layers + 1, 2, width, width), f32),
            pltpu.VMEM((2 * layers + 1, 2, width, width), f32),
            pltpu.VMEM(wave, f32),
            pltpu.VMEM(strips, f32),
            pltpu.VMEM(strips, f32),
            pltpu.VMEM(wave, f32),
            pltpu.VMEM(wave, f32),
            pltpu.VMEM((2, 2, 8, half), jnp.int32),
        ]
        + [pairs] * 2
        + [quads] * 4
        + [pairs] * 2
        + [two] * 2
        + [square] * 4
        + [windows] * 2
        + [two],
        compiler_params=pltpu.CompilerParams(
            collective_id=0, has_side_effects=True, vmem_limit_bytes=48 * 1024 * 1024
        ),
    )(object_field, illumination, pos, measured.reshape(width, width), tables)


def solution(mesh):
    placed = (
        P("sl", None, "tx", "ty"),
        P(),
        P("tx", "ty", None, None),
        P("tx", "ty", None, None, None),
    )
    return jax.shard_map(
        body, mesh=mesh, in_specs=placed, out_specs=P("sl", None, "tx", "ty"), check_vma=False
    )
```
